32 devices in a mesh: rep: 16 (over z, y, x), section: 2 (over core).
Axes of the slice: x: 2, y: 2, z: 4, core: 2. Of those that a mesh axis runs over, the one named last changes fastest.
Arguments:
- ends: bfloat16 [2, 16, 2, 128, 1024], P('section', 'rep'), may hold values from -6 to 6
- w_gate: bfloat16 [2, 16, 1024, 256], P('section', 'rep'), may hold values from -6 to 6
- w_up: bfloat16 [2, 16, 1024, 256], P('section', 'rep'), may hold values from -6 to 6
- slow_down: bfloat16 [2, 16, 256, 1024], P('section', 'rep'), may hold values from -6 to 6
- adam_m: bfloat16 [2, 16, 256, 1024], P('section', 'rep'), may hold values from -2 to 2
- adam_v: bfloat16 [2, 16, 256, 1024], P('section', 'rep'), may hold values from 0.019897461 to 0.19921875
- momentum: bfloat16 [2, 16, 256, 1024], P('section', 'rep'), may hold values from -6 to 6
- routes: int32 [2, 16], replicated, may hold values from 0 to 15, as said below
- partner: int32 [16], replicated, may hold values from 0 to 15, as said below
Outputs:
- new_slow: bfloat16 [2, 16, 256, 1024], P('section', 'rep')
- new_momentum: bfloat16 [2, 16, 256, 1024], P('section', 'rep')
The draws below stay inside these ranges and needn't reach their ends.
Inputs may be any that keep to these rules, and one draw needn't show every extreme that they name: For each micro-batch b there is one number k_b with 1 <= k_b < 16, and routes[b, r] is r with the bits of k_b flipped (bitwise exclusive or). partner[r] is r with the bits of one number of 1 to 3 flipped, the same number for the four replicas of each aligned group of four, so partner[partner[r]] = r.
All inputs are finite; a program needn't handle non-finite values.
Results may differ from the reference program's by a relative error of at most 0.0036.
Values may be sent and summed in bfloat16 or wider, within the bound.
A program may use at most 64 MiB of HBM per device.

```python
import math
import jax
import jax.numpy as jnp
from jax import lax

D = 1024
H = 256
ROWS = 128
MB = 2
REP = 16
SECTIONS = 2


def draw_routes(key, part):
    route_keys = jax.random.randint(jax.random.fold_in(key, 11), (MB,), 1, REP, dtype=jnp.int32)
    replica_ids = jnp.arange(REP, dtype=jnp.int32)
    return jnp.bitwise_xor(replica_ids[None, :], route_keys[:, None]).astype(jnp.int32)


def draw_partner(key, part):
    group_flips = jax.random.randint(jax.random.fold_in(key, 23), (REP // 4,), 1, 4, dtype=jnp.int32)
    replica_ids = jnp.arange(REP, dtype=jnp.int32)
    return jnp.bitwise_xor(replica_ids, group_flips[replica_ids // 4]).astype(jnp.int32)


def steps_of(rng, dims, shards, least, high):
    level, own = 1.0, jax.random.fold_in(rng, 6)
    for dim, parts in shards:
        draws = jnp.exp(jax.random.uniform(jax.random.fold_in(own, dim), (parts,), jnp.float32, least / len(shards), high / len(shards)))
        level = level * jnp.repeat(draws, dims[dim] // parts).reshape([-1 if axis == dim else 1 for axis in range(len(dims))])
    return level


def noise(stream_key, extent, width, bound, shards=(), kind=jnp.bfloat16):
    factor_of = steps_of(stream_key, extent, shards, -0.22, 0.18) if shards else 1.0
    entries = jax.random.normal(stream_key, extent, jnp.float32) * width * factor_of
    return jnp.minimum(jnp.maximum(entries, -bound), bound).astype(kind)


def setup_inputs(seed: int = 0) -> dict:
    streams_of = jax.random.split(jax.random.key(seed), 10)
    return {
        "ends": noise(streams_of[0], (SECTIONS, REP, MB, ROWS, D), 1.0, 6.0, ((0, 2), (1, 16))),
        "w_gate": noise(streams_of[1], (SECTIONS, REP, D, H), 1.0, 6.0, ((0, 2), (1, 16))),
        "w_up": noise(streams_of[2], (SECTIONS, REP, D, H), 1.0, 6.0, ((0, 2), (1, 16))),
        "slow_down": noise(streams_of[3], (SECTIONS, REP, H, D), 1.0, 6.0, ((0, 2), (1, 16))),
        "adam_m": noise(streams_of[4], (SECTIONS, REP, H, D), 0.15, 2.0, ((0, 2), (1, 16))),
        "adam_v": jnp.clip(jnp.exp(math.log(0.19921875) - 2.3038113 * jax.random.uniform(streams_of[5], (SECTIONS, REP, H, D), jnp.float32) ** steps_of(streams_of[5], (SECTIONS, REP, H, D), ((0, 2), (1, 16)), -0.2, 0.2)), 0.019897461, 0.19921875).astype(jnp.bfloat16),
        "momentum": noise(streams_of[6], (SECTIONS, REP, H, D), 1.0, 6.0, ((0, 2), (1, 16))),
        "routes": draw_routes(jax.random.fold_in(streams_of[9], 71), 0),
        "partner": draw_partner(jax.random.fold_in(streams_of[9], 71), 0),
    }


def forward_rows(in_rows, w_gate, w_up, w_down):
    model_width = in_rows.shape[1]
    hidden_units = w_gate.shape[1]
    as_float = in_rows.astype(jnp.float32)
    row_scale = lax.rsqrt(lax.optimization_barrier(jnp.mean(as_float * as_float, axis=1, keepdims=True)) + 1e-06)
    normed = (as_float * row_scale).astype(jnp.bfloat16)
    gate_act = jnp.dot(normed, w_gate, preferred_element_type=jnp.float32) * model_width ** (-0.5)
    up_act = jnp.dot(normed, w_up, preferred_element_type=jnp.float32) * model_width ** (-0.5)
    hidden = (jax.nn.silu(gate_act) * up_act).astype(jnp.bfloat16)
    branch = jnp.dot(hidden, w_down, preferred_element_type=jnp.float32) * hidden_units ** (-0.5)
    result = (as_float + branch).astype(jnp.bfloat16)
    return (result, (row_scale, gate_act, up_act, hidden))

def backward_rows(cotangent, in_rows, saved_state, w_gate, w_up, w_down):
    row_scale, gate_act, up_act, hidden = saved_state
    model_width = in_rows.shape[1]
    hidden_units = w_gate.shape[1]
    d_hidden = jnp.dot(cotangent, w_down.T, preferred_element_type=jnp.float32) * hidden_units ** (-0.5)
    grad_term = jnp.dot(hidden.T, cotangent, preferred_element_type=jnp.float32) * hidden_units ** (-0.5)
    sigmoid_gate = jax.nn.sigmoid(gate_act)
    d_gate = (d_hidden * up_act * sigmoid_gate * (1.0 + gate_act * (1.0 - sigmoid_gate))).astype(jnp.bfloat16)
    d_up = (d_hidden * gate_act * sigmoid_gate).astype(jnp.bfloat16)
    d_normed = (jnp.dot(d_gate, w_gate.T, preferred_element_type=jnp.float32) + jnp.dot(d_up, w_up.T, preferred_element_type=jnp.float32)) * model_width ** (-0.5)
    as_float = in_rows.astype(jnp.float32)
    back_rows = cotangent.astype(jnp.float32) + row_scale * d_normed - as_float * row_scale ** 3 * lax.optimization_barrier(jnp.mean(d_normed * as_float, axis=1, keepdims=True))
    return (grad_term, back_rows.astype(jnp.bfloat16))

def grad_only(cotangent, saved_state, w_down):
    row_scale, gate_act, up_act, hidden = saved_state
    hidden_units = w_down.shape[0]
    return jnp.dot(hidden.T, cotangent, preferred_element_type=jnp.float32) * hidden_units ** (-0.5)

def reference(ends, w_gate, w_up, slow_down, adam_m, adam_v, momentum, routes, partner):
    count_rep = ends.shape[1]
    micro_count = ends.shape[2]
    rows_each = ends.shape[3]
    model_width = ends.shape[4]
    hidden_units = w_gate.shape[3]

    def flatten(stacked):
        return stacked.reshape(count_rep, micro_count * rows_each, model_width)

    def unflatten(stacked):
        return stacked.reshape(count_rep, micro_count, rows_each, model_width)

    def first_forward(operands):
        in_rows, gate_w, up_w, down_w = operands
        return forward_rows(in_rows, gate_w, up_w, down_w)
    sent_rows, first_saved = lax.map(first_forward, (flatten(ends[0]), w_gate[0], w_up[0], slow_down[0]))
    replica_ids = jnp.arange(count_rep, dtype=jnp.int32)
    batch_ids = jnp.arange(micro_count, dtype=jnp.int32)
    inverse = jnp.zeros((micro_count, count_rep), jnp.int32).at[batch_ids[:, None], routes].set(jnp.broadcast_to(replica_ids[None, :], (micro_count, count_rep)))
    arrived = unflatten(sent_rows)[inverse.T, batch_ids[None, :]]

    def last_step(operands):
        in_rows, cotangent, gate_w, up_w, down_w = operands
        result, saved_state = forward_rows(in_rows, gate_w, up_w, down_w)
        return backward_rows(cotangent, in_rows, saved_state, gate_w, up_w, down_w)
    last_grad, back_rows = lax.map(last_step, (flatten(arrived), flatten(ends[1]), w_gate[1], w_up[1], slow_down[1]))
    returned = unflatten(back_rows)[routes.T, batch_ids[None, :]]

    def first_back(operands):
        cotangent, row_scale, gate_act, up_act, hidden, down_w = operands
        return grad_only(cotangent, (row_scale, gate_act, up_act, hidden), down_w)
    first_grad = lax.map(first_back, (flatten(returned),) + tuple(first_saved) + (slow_down[0],))
    grads = jnp.stack([first_grad, last_grad]).reshape(2 * count_rep, hidden_units, model_width)

    def adam_step(operands):
        grad_sum, first_in, second_in, slow_in = operands
        first_moment = 0.9 * first_in.astype(jnp.float32) + 0.1 * grad_sum
        second_moment = 0.999 * second_in.astype(jnp.float32) + 0.001 * grad_sum * grad_sum
        update = first_moment / (jnp.sqrt(second_moment) + 1e-08)
        return (update + 0.1 * slow_in.astype(jnp.float32)).astype(jnp.bfloat16)
    flat_shape = (2 * count_rep, hidden_units, model_width)
    pseudo = lax.map(adam_step, (grads, adam_m.reshape(flat_shape), adam_v.reshape(flat_shape), slow_down.reshape(flat_shape)))
    pseudo = pseudo.reshape(2, count_rep, hidden_units, model_width)

    def outer_step(replica):
        mate = partner[replica]
        mean_pseudo = 0.5 * (pseudo[:, replica].astype(jnp.float32) + pseudo[:, mate].astype(jnp.float32))
        moment = 0.9 * momentum[:, replica].astype(jnp.float32) + mean_pseudo
        averaged = 0.5 * (slow_down[:, replica].astype(jnp.float32) + slow_down[:, mate].astype(jnp.float32))
        updated = averaged - 0.014 * (0.9 * moment + mean_pseudo)
        return (updated.astype(jnp.bfloat16), moment.astype(jnp.bfloat16))
    new_slow, new_momentum = lax.map(outer_step, replica_ids)
    return (jnp.swapaxes(new_slow, 0, 1), jnp.swapaxes(new_momentum, 0, 1))
```

```python
import jax
import jax.numpy as jnp
from jax import lax
from jax.sharding import PartitionSpec as P


def partner_2(x, axis, bit):
    return lax.ppermute(x, axis, [(i, i ^ 1 << bit) for i in range(lax.axis_size(axis))])


def forward_rows(in_rows, w_gate, w_up, w_down):
    model_width = in_rows.shape[1]
    hidden_units = w_gate.shape[1]
    as_float = in_rows.astype(jnp.float32)
    row_scale = lax.rsqrt(jnp.mean(as_float * as_float, axis=1, keepdims=True) + 1e-06)
    normed = (as_float * row_scale).astype(jnp.bfloat16)
    gate_act = jnp.dot(normed, w_gate, preferred_element_type=jnp.float32) * model_width ** (-0.5)
    up_act = jnp.dot(normed, w_up, preferred_element_type=jnp.float32) * model_width ** (-0.5)
    hidden = (jax.nn.silu(gate_act) * up_act).astype(jnp.bfloat16)
    branch = jnp.dot(hidden, w_down, preferred_element_type=jnp.float32) * hidden_units ** (-0.5)
    result = (as_float + branch).astype(jnp.bfloat16)
    return (result, (row_scale, gate_act, up_act, hidden))


def contract_last(left, right):
    return lax.dot_general(
        left, right, (((1,), (1,)), ((), ())), preferred_element_type=jnp.float32
    )


def grad_rows(cotangent, hidden, hidden_units):
    return lax.dot_general(
        hidden, cotangent, (((0,), (0,)), ((), ())), preferred_element_type=jnp.float32
    ) * hidden_units ** (-0.5)


def backward_rows(cotangent, in_rows, saved_state, w_gate, w_up, w_down):
    row_scale, gate_act, up_act, hidden = saved_state
    model_width = in_rows.shape[1]
    hidden_units = w_gate.shape[1]
    d_hidden = contract_last(cotangent, w_down) * hidden_units ** (-0.5)
    grad_term = grad_rows(cotangent, hidden, hidden_units)
    sigmoid_gate = jax.nn.sigmoid(gate_act)
    d_gate = (d_hidden * up_act * sigmoid_gate * (1.0 + gate_act * (1.0 - sigmoid_gate))).astype(
        jnp.bfloat16
    )
    d_up = (d_hidden * gate_act * sigmoid_gate).astype(jnp.bfloat16)
    d_normed = (contract_last(d_gate, w_gate) + contract_last(d_up, w_up)) * model_width ** (-0.5)
    as_float = in_rows.astype(jnp.float32)
    back_rows = (
        cotangent.astype(jnp.float32)
        + row_scale * d_normed
        - as_float * row_scale**3 * jnp.mean(d_normed * as_float, axis=1, keepdims=True)
    )
    return (grad_term, back_rows.astype(jnp.bfloat16))


def send_rows(payload, flip_key, source):
    replicas = lax.axis_size("rep")
    bits = replicas.bit_length() - 1
    starts = list(range(0, bits, 4))
    for start in starts:
        width = min(4, bits - start)
        target = 1 - source if start == starts[-1] else source

        def branch(flip, start=start, target=target):
            pairs = [
                (2 * r + source, 2 * (r ^ flip << start) + target) for r in range(replicas)
            ]

            def run(rows):
                if target == source and flip == 0:
                    return rows
                return lax.ppermute(rows, ("rep", "section"), pairs)

            return run

        payload = lax.switch(
            flip_key >> start & (1 << width) - 1, [branch(f) for f in range(1 << width)], payload
        )
    return payload


def pair_values(values, flip_bits):
    for bit_index in range(2):
        other_values = partner_2(values, "rep", bit_index)
        values = jnp.where(flip_bits >> bit_index & 1 == 1, other_values, values)
    return values


def on_device(ends, w_gate, w_up, slow_down, adam_m, adam_v, momentum, routes, partner):
    micro_count, row_count, model_width = ends.shape[2:]
    own_data = ends.reshape(micro_count * row_count, model_width)
    gate_w = w_gate[0, 0]
    up_w = w_up[0, 0]
    down_w = slow_down[0, 0]
    hidden_units = gate_w.shape[1]
    replica = lax.axis_index("rep")
    on_first = lax.axis_index("section") == 0
    flip_keys = routes[:, 0]
    flip_bits = jnp.bitwise_xor(partner[replica], replica)
    partner_slow = pair_values(down_w, flip_bits)

    def cut(rows):
        return rows.reshape(micro_count, row_count, model_width)

    def first_forward():
        result, saved = forward_rows(own_data, gate_w, up_w, down_w)
        return result, saved[3]

    def first_idle():
        return own_data, jnp.zeros((own_data.shape[0], hidden_units), jnp.bfloat16)

    sent, hidden = lax.cond(on_first, first_forward, first_idle)
    sent = cut(sent)
    arrived = jnp.concatenate([send_rows(sent[b], flip_keys[b], 0) for b in range(micro_count)])

    def last_work():
        result, saved = forward_rows(arrived, gate_w, up_w, down_w)
        term, back = backward_rows(own_data, arrived, saved, gate_w, up_w, down_w)
        return term, back

    def last_idle():
        return jnp.zeros((hidden_units, model_width), jnp.float32), own_data

    last_term, back = lax.cond(on_first, last_idle, last_work)
    back = cut(back)
    returned = jnp.concatenate([send_rows(back[b], flip_keys[b], 1) for b in range(micro_count)])
    grad_sum = lax.cond(
        on_first, lambda: grad_rows(returned, hidden, hidden_units), lambda: last_term
    )
    first_moment = 0.9 * adam_m[0, 0].astype(jnp.float32) + 0.1 * grad_sum
    second_moment = 0.999 * adam_v[0, 0].astype(jnp.float32) + 0.001 * grad_sum * grad_sum
    slow_float = down_w.astype(jnp.float32)
    pseudo = (first_moment / (jnp.sqrt(second_moment) + 1e-08) + 0.1 * slow_float).astype(
        jnp.bfloat16
    )
    partner_pseudo = pair_values(pseudo, flip_bits)
    mean_pseudo = 0.5 * (pseudo.astype(jnp.float32) + partner_pseudo.astype(jnp.float32))
    momentum_float = 0.9 * momentum[0, 0].astype(jnp.float32) + mean_pseudo
    new_slow = 0.5 * (slow_float + partner_slow.astype(jnp.float32)) - 0.014 * (
        0.9 * momentum_float + mean_pseudo
    )
    return (
        new_slow.astype(jnp.bfloat16)[None, None],
        momentum_float.astype(jnp.bfloat16)[None, None],
    )


def solution(mesh):
    placed = (
        P("section", "rep", None, None, None),
        P("section", "rep", None, None),
        P("section", "rep", None, None),
        P("section", "rep", None, None),
        P("section", "rep", None, None),
        P("section", "rep", None, None),
        P("section", "rep", None, None),
        P(),
        P(),
    )
    return jax.shard_map(
        on_device,
        mesh=mesh,
        in_specs=placed,
        out_specs=(P("section", "rep", None, None), P("section", "rep", None, None)),
        check_vma=False,
    )
```

```python
import functools

import jax
import jax.numpy as jnp
from jax import lax
from jax.experimental import pallas as pl
from jax.experimental.pallas import tpu as pltpu
from jax.sharding import PartitionSpec as P


def partner_2(x, axis, bit):
    return lax.ppermute(x, axis, [(i, i ^ 1 << bit) for i in range(lax.axis_size(axis))])


def forward_rows(in_rows, w_gate, w_up, w_down):
    model_width = in_rows.shape[1]
    hidden_units = w_gate.shape[1]
    as_float = in_rows.astype(jnp.float32)
    row_scale = lax.rsqrt(jnp.mean(as_float * as_float, axis=1, keepdims=True) + 1e-06)
    normed = (as_float * row_scale).astype(jnp.bfloat16)
    gate_act = jnp.dot(normed, w_gate, preferred_element_type=jnp.float32) * model_width ** (-0.5)
    up_act = jnp.dot(normed, w_up, preferred_element_type=jnp.float32) * model_width ** (-0.5)
    hidden = (jax.nn.silu(gate_act) * up_act).astype(jnp.bfloat16)
    branch = jnp.dot(hidden, w_down, preferred_element_type=jnp.float32) * hidden_units ** (-0.5)
    result = (as_float + branch).astype(jnp.bfloat16)
    return (result, (row_scale, gate_act, up_act, hidden))


def contract_last(left, right):
    return lax.dot_general(
        left, right, (((1,), (1,)), ((), ())), preferred_element_type=jnp.float32
    )


def grad_rows(cotangent, hidden, hidden_units):
    return lax.dot_general(
        hidden, cotangent, (((0,), (0,)), ((), ())), preferred_element_type=jnp.float32
    ) * hidden_units ** (-0.5)


def backward_rows(cotangent, in_rows, saved_state, w_gate, w_up, w_down):
    row_scale, gate_act, up_act, hidden = saved_state
    model_width = in_rows.shape[1]
    hidden_units = w_gate.shape[1]
    d_hidden = contract_last(cotangent, w_down) * hidden_units ** (-0.5)
    grad_term = grad_rows(cotangent, hidden, hidden_units)
    sigmoid_gate = jax.nn.sigmoid(gate_act)
    d_gate = (d_hidden * up_act * sigmoid_gate * (1.0 + gate_act * (1.0 - sigmoid_gate))).astype(
        jnp.bfloat16
    )
    d_up = (d_hidden * gate_act * sigmoid_gate).astype(jnp.bfloat16)
    d_normed = (contract_last(d_gate, w_gate) + contract_last(d_up, w_up)) * model_width ** (-0.5)
    as_float = in_rows.astype(jnp.float32)
    back_rows = (
        cotangent.astype(jnp.float32)
        + row_scale * d_normed
        - as_float * row_scale**3 * jnp.mean(d_normed * as_float, axis=1, keepdims=True)
    )
    return (grad_term, back_rows.astype(jnp.bfloat16))


def send_rows(payload, flip_key, source):
    replicas = lax.axis_size("rep")
    bits = replicas.bit_length() - 1
    starts = list(range(0, bits, 4))
    for start in starts:
        width = min(4, bits - start)
        target = 1 - source if start == starts[-1] else source

        def branch(flip, start=start, target=target):
            pairs = [
                (2 * r + source, 2 * (r ^ flip << start) + target) for r in range(replicas)
            ]

            def run(rows):
                if target == source and flip == 0:
                    return rows
                return lax.ppermute(rows, ("rep", "section"), pairs)

            return run

        payload = lax.switch(
            flip_key >> start & (1 << width) - 1, [branch(f) for f in range(1 << width)], payload
        )
    return payload


def outer_kernel(
    chunks, masks, grad, first_in, second_in, slow, mate_slow, momentum,
    new_slow, new_momentum, own, near, chosen, far, send_near, recv_near, send_far, recv_far,
):
    me = lax.axis_index("rep")
    peers = (me + 1 - 2 * (me % 2), me + 2 - 4 * ((me // 2) % 2))
    rows = grad.shape[0] // chunks
    f32, bf16 = jnp.float32, jnp.bfloat16

    barrier = pltpu.get_barrier_semaphore()
    for peer in peers:
        pl.semaphore_signal(
            barrier, inc=1, device_id={"rep": peer}, device_id_type=pl.DeviceIdType.MESH
        )

    def part(c):
        return pl.ds(pl.multiple_of(c * rows, rows), rows)

    def near_copy(c):
        return pltpu.make_async_remote_copy(
            src_ref=own.at[part(c)], dst_ref=near.at[part(c)],
            send_sem=send_near.at[c], recv_sem=recv_near.at[c],
            device_id={"rep": peers[0]}, device_id_type=pl.DeviceIdType.MESH,
        )

    def far_copy(c):
        return pltpu.make_async_remote_copy(
            src_ref=chosen.at[part(c)], dst_ref=far.at[part(c)],
            send_sem=send_far.at[c], recv_sem=recv_far.at[c],
            device_id={"rep": peers[1]}, device_id_type=pl.DeviceIdType.MESH,
        )

    def adam(c):
        p = part(c)
        g = grad[p, :]
        first = 0.9 * first_in[p, :].astype(f32) + 0.1 * g
        second = 0.999 * second_in[p, :].astype(f32) + 0.001 * g * g
        step = first / (jnp.sqrt(second) + 1e-08)
        own[p, :] = (step + 0.1 * slow[p, :].astype(f32)).astype(bf16)

    adam(0)
    pl.semaphore_wait(barrier, 2)
    near_copy(0).start()

    def begin(c, carry):
        adam(c)
        near_copy(c).start()
        return carry

    lax.fori_loop(1, chunks, begin, 0)

    def pass_on(c):
        p = part(c)
        near_copy(c).wait_recv()
        chosen[p, :] = jnp.where(
            masks[0:1, :] == 1, near[p, :].astype(f32), own[p, :].astype(f32)
        ).astype(bf16)
        far_copy(c).start()

    def finish(c):
        p = part(c)
        far_copy(c).wait_recv()
        mate = jnp.where(masks[1:2, :] == 1, far[p, :].astype(f32), chosen[p, :].astype(f32))
        mean = 0.5 * (own[p, :].astype(f32) + mate)
        moment = 0.9 * momentum[p, :].astype(f32) + mean
        averaged = 0.5 * (slow[p, :].astype(f32) + mate_slow[p, :].astype(f32))
        new_slow[p, :] = (averaged - 0.014 * (0.9 * moment + mean)).astype(bf16)
        new_momentum[p, :] = moment.astype(bf16)

    lag = 2

    def steady(c, carry):
        pass_on(c)

        @pl.when(c >= lag)
        def _():
            finish(c - lag)

        return carry

    lax.fori_loop(0, chunks, steady, 0)

    def drain(c, carry):
        finish(c)
        return carry

    lax.fori_loop(chunks - lag, chunks, drain, 0)

    def settle(c, carry):
        near_copy(c).wait_send()
        far_copy(c).wait_send()
        return carry

    lax.fori_loop(0, chunks, settle, 0)


def outer_update(masks, grad, first_in, second_in, slow, mate_slow, momentum):
    hidden_units, model_width = grad.shape
    chunks = hidden_units // 16
    block = pltpu.VMEM((hidden_units, model_width), jnp.bfloat16)
    sems = pltpu.SemaphoreType.DMA((chunks,))
    out = jax.ShapeDtypeStruct((hidden_units, model_width), jnp.bfloat16)
    in_vmem = pl.BlockSpec(memory_space=pltpu.VMEM)
    return pl.pallas_call(
        functools.partial(outer_kernel, chunks),
        out_shape=(out, out),
        in_specs=[in_vmem] * 7,
        out_specs=(in_vmem, in_vmem),
        scratch_shapes=[block] * 4 + [sems] * 4,
        compiler_params=pltpu.CompilerParams(
            collective_id=0, has_side_effects=True, vmem_limit_bytes=16 * 1024 * 1024
        ),
        name="outer",
    )(masks, grad, first_in, second_in, slow, mate_slow, momentum)


def on_device(ends, w_gate, w_up, slow_down, adam_m, adam_v, momentum, routes, partner):
    micro_count, row_count, model_width = ends.shape[2:]
    own_data = ends.reshape(micro_count * row_count, model_width)
    gate_w = w_gate[0, 0]
    up_w = w_up[0, 0]
    down_w = slow_down[0, 0]
    hidden_units = gate_w.shape[1]
    replica = lax.axis_index("rep")
    on_first = lax.axis_index("section") == 0
    flip_keys = routes[:, 0]
    flip_bits = jnp.bitwise_xor(partner[replica], replica)
    near_slow = partner_2(down_w, "rep", 0)

    def cut(rows):
        return rows.reshape(micro_count, row_count, model_width)

    def first_forward():
        result, saved = forward_rows(own_data, gate_w, up_w, down_w)
        return result, saved[3]

    def first_idle():
        return own_data, jnp.zeros((own_data.shape[0], hidden_units), jnp.bfloat16)

    sent, hidden = lax.cond(on_first, first_forward, first_idle)
    sent = cut(sent)
    arrived = [send_rows(sent[b], flip_keys[b], 0) for b in range(micro_count)]
    near_slow, *arrived = lax.optimization_barrier((near_slow, *arrived))
    arrived = jnp.concatenate(arrived)
    chosen_slow = jnp.where(flip_bits & 1 == 1, near_slow, down_w)
    far_slow = partner_2(chosen_slow, "rep", 1)

    def last_work():
        _, saved = forward_rows(arrived, gate_w, up_w, down_w)
        term, back = backward_rows(own_data, arrived, saved, gate_w, up_w, down_w)
        return term, back

    def last_idle():
        return jnp.zeros((hidden_units, model_width), jnp.float32), own_data

    last_term, back = lax.cond(on_first, last_idle, last_work)
    back = cut(back)
    returned = [send_rows(back[b], flip_keys[b], 1) for b in range(micro_count)]
    far_slow, *returned = lax.optimization_barrier((far_slow, *returned))
    returned = jnp.concatenate(returned)
    partner_slow = jnp.where(flip_bits >> 1 & 1 == 1, far_slow, chosen_slow)
    grad_sum = lax.cond(
        on_first, lambda: grad_rows(returned, hidden, hidden_units), lambda: last_term
    )
    masks = jnp.zeros((8, model_width), jnp.int32)
    masks = masks.at[0].set(flip_bits & 1).at[1].set(flip_bits >> 1 & 1)
    new_slow, new_momentum = outer_update(
        masks, grad_sum, adam_m[0, 0], adam_v[0, 0], down_w, partner_slow, momentum[0, 0]
    )
    return new_slow[None, None], new_momentum[None, None]


def solution(mesh):
    placed = (
        P("section", "rep", None, None, None),
        P("section", "rep", None, None),
        P("section", "rep", None, None),
        P("section", "rep", None, None),
        P("section", "rep", None, None),
        P("section", "rep", None, None),
        P("section", "rep", None, None),
        P(),
        P(),
    )

    return jax.shard_map(
        on_device,
        mesh=mesh,
        in_specs=placed,
        out_specs=(P("section", "rep", None, None), P("section", "rep", None, None)),
        check_vma=False,
    )
```

```python
import functools

import jax
import jax.numpy as jnp
from jax import lax
from jax.experimental import pallas as pl
from jax.experimental.pallas import tpu as pltpu
from jax.sharding import PartitionSpec as P


def partner_2(x, axis, bit):
    return lax.ppermute(x, axis, [(i, i ^ 1 << bit) for i in range(lax.axis_size(axis))])


def forward_rows(in_rows, w_gate, w_up, w_down):
    model_width = in_rows.shape[1]
    hidden_units = w_gate.shape[1]
    as_float = in_rows.astype(jnp.float32)
    row_scale = lax.rsqrt(jnp.mean(as_float * as_float, axis=1, keepdims=True) + 1e-06)
    normed = (as_float * row_scale).astype(jnp.bfloat16)
    gate_act = jnp.dot(normed, w_gate, preferred_element_type=jnp.float32) * model_width ** (-0.5)
    up_act = jnp.dot(normed, w_up, preferred_element_type=jnp.float32) * model_width ** (-0.5)
    hidden = (jax.nn.silu(gate_act) * up_act).astype(jnp.bfloat16)
    branch = jnp.dot(hidden, w_down, preferred_element_type=jnp.float32) * hidden_units ** (-0.5)
    result = (as_float + branch).astype(jnp.bfloat16)
    return (result, (row_scale, gate_act, up_act, hidden))


def contract_last(left, right):
    return lax.dot_general(
        left, right, (((1,), (1,)), ((), ())), preferred_element_type=jnp.float32
    )


def grad_rows(cotangent, hidden, hidden_units):
    return lax.dot_general(
        hidden, cotangent, (((0,), (0,)), ((), ())), preferred_element_type=jnp.float32
    ) * hidden_units ** (-0.5)


def backward_rows(cotangent, in_rows, saved_state, w_gate, w_up, w_down):
    row_scale, gate_act, up_act, hidden = saved_state
    model_width = in_rows.shape[1]
    hidden_units = w_gate.shape[1]
    d_hidden = contract_last(cotangent, w_down) * hidden_units ** (-0.5)
    grad_term = grad_rows(cotangent, hidden, hidden_units)
    sigmoid_gate = jax.nn.sigmoid(gate_act)
    d_gate = (d_hidden * up_act * sigmoid_gate * (1.0 + gate_act * (1.0 - sigmoid_gate))).astype(
        jnp.bfloat16
    )
    d_up = (d_hidden * gate_act * sigmoid_gate).astype(jnp.bfloat16)
    d_normed = (contract_last(d_gate, w_gate) + contract_last(d_up, w_up)) * model_width ** (-0.5)
    as_float = in_rows.astype(jnp.float32)
    back_rows = (
        cotangent.astype(jnp.float32)
        + row_scale * d_normed
        - as_float * row_scale**3 * jnp.mean(d_normed * as_float, axis=1, keepdims=True)
    )
    return (grad_term, back_rows.astype(jnp.bfloat16))


def send_rows(payload, flip_key, source):
    replicas = lax.axis_size("rep")
    bits = replicas.bit_length() - 1
    starts = list(range(0, bits, 4))
    for start in starts:
        width = min(4, bits - start)
        target = 1 - source if start == starts[-1] else source

        def branch(flip, start=start, target=target):
            pairs = [
                (2 * r + source, 2 * (r ^ flip << start) + target) for r in range(replicas)
            ]

            def run(rows):
                if target == source and flip == 0:
                    return rows
                return lax.ppermute(rows, ("rep", "section"), pairs)

            return run

        payload = lax.switch(
            flip_key >> start & (1 << width) - 1, [branch(f) for f in range(1 << width)], payload
        )
    return payload


def outer_kernel(
    chunks, masks, grad, first_in, second_in, slow, mate_slow, momentum,
    new_slow, new_momentum, own, near, chosen, far, send_near, recv_near, send_far, recv_far,
):
    me = lax.axis_index("rep")
    peers = (me + 1 - 2 * (me % 2), me + 2 - 4 * ((me // 2) % 2))
    rows = grad.shape[0] // chunks
    f32, bf16 = jnp.float32, jnp.bfloat16

    barrier = pltpu.get_barrier_semaphore()
    for peer in peers:
        pl.semaphore_signal(
            barrier, inc=1, device_id={"rep": peer}, device_id_type=pl.DeviceIdType.MESH
        )

    def part(c):
        return pl.ds(pl.multiple_of(c * rows, rows), rows)

    def near_copy(c, order):
        return pltpu.make_async_remote_copy(
            src_ref=own.at[part(c)], dst_ref=near.at[part(c)],
            send_sem=send_near.at[c], recv_sem=recv_near.at[c],
            device_id={"rep": peers[order]}, device_id_type=pl.DeviceIdType.MESH,
        )

    def far_copy(c, order):
        return pltpu.make_async_remote_copy(
            src_ref=chosen.at[part(c)], dst_ref=far.at[part(c)],
            send_sem=send_far.at[c], recv_sem=recv_far.at[c],
            device_id={"rep": peers[1 - order]}, device_id_type=pl.DeviceIdType.MESH,
        )

    def adam(c):
        p = part(c)
        g = grad[p, :]
        first = 0.9 * first_in[p, :].astype(f32) + 0.1 * g
        second = 0.999 * second_in[p, :].astype(f32) + 0.001 * g * g
        step = first / (jnp.sqrt(second) + 1e-08)
        own[p, :] = (step + 0.1 * slow[p, :].astype(f32)).astype(bf16)

    def send(c, order):
        near_copy(c, order).start()

    def begin(c, order):
        adam(c)
        send(c, order)

    def pass_on(c, order):
        p = part(c)
        near_copy(c, order).wait_recv()
        chosen[p, :] = jnp.where(
            masks[order : order + 1, :] == 1, near[p, :].astype(f32), own[p, :].astype(f32)
        ).astype(bf16)
        far_copy(c, order).start()

    def finish(c, order):
        p = part(c)
        far_copy(c, order).wait_recv()
        mate = jnp.where(
            masks[1 - order : 2 - order, :] == 1, far[p, :].astype(f32), chosen[p, :].astype(f32)
        )
        mean = 0.5 * (own[p, :].astype(f32) + mate)
        moment = 0.9 * momentum[p, :].astype(f32) + mean
        averaged = 0.5 * (slow[p, :].astype(f32) + mate_slow[p, :].astype(f32))
        new_slow[p, :] = (averaged - 0.014 * (0.9 * moment + mean)).astype(bf16)
        new_momentum[p, :] = moment.astype(bf16)

    def settle(c, order):
        near_copy(c, order).wait_send()
        far_copy(c, order).wait_send()

    def both(start, stop, *stages):
        def run(pair, carry):
            for stage in stages:
                for order in range(2):
                    stage(2 * pair + order, order)
            return carry

        lax.fori_loop(start, stop, run, 0)

    pairs = chunks // 2
    both(0, 1, lambda c, order: adam(c))
    pl.semaphore_wait(barrier, 2)
    both(0, 1, send)
    both(1, pairs, begin)
    both(0, 1, pass_on)
    both(1, pairs, pass_on, lambda c, order: finish(c - 2, order))
    both(pairs - 1, pairs, finish)
    both(0, pairs, settle)


def outer_update(masks, grad, first_in, second_in, slow, mate_slow, momentum):
    hidden_units, model_width = grad.shape
    chunks = hidden_units // 32
    block = pltpu.VMEM((hidden_units, model_width), jnp.bfloat16)
    sems = pltpu.SemaphoreType.DMA((chunks,))
    out = jax.ShapeDtypeStruct((hidden_units, model_width), jnp.bfloat16)
    in_vmem = pl.BlockSpec(memory_space=pltpu.VMEM)
    return pl.pallas_call(
        functools.partial(outer_kernel, chunks),
        out_shape=(out, out),
        in_specs=[in_vmem] * 7,
        out_specs=(in_vmem, in_vmem),
        scratch_shapes=[block] * 4 + [sems] * 4,
        compiler_params=pltpu.CompilerParams(
            collective_id=0, has_side_effects=True, vmem_limit_bytes=16 * 1024 * 1024
        ),
        name="outer",
    )(masks, grad, first_in, second_in, slow, mate_slow, momentum)


def on_device(ends, w_gate, w_up, slow_down, adam_m, adam_v, momentum, routes, partner):
    micro_count, row_count, model_width = ends.shape[2:]
    own_data = ends.reshape(micro_count * row_count, model_width)
    gate_w = w_gate[0, 0]
    up_w = w_up[0, 0]
    down_w = slow_down[0, 0]
    hidden_units = gate_w.shape[1]
    replica = lax.axis_index("rep")
    on_first = lax.axis_index("section") == 0
    flip_keys = routes[:, 0]
    flip_bits = jnp.bitwise_xor(partner[replica], replica)
    near_slow = partner_2(down_w, "rep", 0)

    def cut(rows):
        return rows.reshape(micro_count, row_count, model_width)

    def first_forward():
        result, saved = forward_rows(own_data, gate_w, up_w, down_w)
        return result, saved[3]

    def first_idle():
        return own_data, jnp.zeros((own_data.shape[0], hidden_units), jnp.bfloat16)

    sent, hidden = lax.cond(on_first, first_forward, first_idle)
    sent = cut(sent)
    arrived = [send_rows(sent[b], flip_keys[b], 0) for b in range(micro_count)]
    near_slow, *arrived = lax.optimization_barrier((near_slow, *arrived))
    arrived = jnp.concatenate(arrived)
    chosen_slow = jnp.where(flip_bits & 1 == 1, near_slow, down_w)
    far_slow = partner_2(chosen_slow, "rep", 1)

    def last_work():
        _, saved = forward_rows(arrived, gate_w, up_w, down_w)
        term, back = backward_rows(own_data, arrived, saved, gate_w, up_w, down_w)
        return term, back

    def last_idle():
        return jnp.zeros((hidden_units, model_width), jnp.float32), own_data

    last_term, back = lax.cond(on_first, last_idle, last_work)
    back = cut(back)
    returned = [send_rows(back[b], flip_keys[b], 1) for b in range(micro_count)]
    far_slow, *returned = lax.optimization_barrier((far_slow, *returned))
    returned = jnp.concatenate(returned)
    partner_slow = jnp.where(flip_bits >> 1 & 1 == 1, far_slow, chosen_slow)
    grad_sum = lax.cond(
        on_first, lambda: grad_rows(returned, hidden, hidden_units), lambda: last_term
    )
    masks = jnp.zeros((8, model_width), jnp.int32)
    masks = masks.at[0].set(flip_bits & 1).at[1].set(flip_bits >> 1 & 1)
    new_slow, new_momentum = outer_update(
        masks, grad_sum, adam_m[0, 0], adam_v[0, 0], down_w, partner_slow, momentum[0, 0]
    )
    return new_slow[None, None], new_momentum[None, None]


def solution(mesh):
    placed = (
        P("section", "rep", None, None, None),
        P("section", "rep", None, None),
        P("section", "rep", None, None),
        P("section", "rep", None, None),
        P("section", "rep", None, None),
        P("section", "rep", None, None),
        P("section", "rep", None, None),
        P(),
        P(),
    )

    return jax.shard_map(
        on_device,
        mesh=mesh,
        in_specs=placed,
        out_specs=(P("section", "rep", None, None), P("section", "rep", None, None)),
        check_vma=False,
    )
```

```python
import functools

import jax
import jax.numpy as jnp
from jax import lax
from jax.experimental import pallas as pl
from jax.experimental.pallas import tpu as pltpu
from jax.sharding import PartitionSpec as P


def partner_2(x, axis, bit):
    return lax.ppermute(x, axis, [(i, i ^ 1 << bit) for i in range(lax.axis_size(axis))])


def forward_rows(in_rows, w_gate, w_up, w_down):
    model_width = in_rows.shape[1]
    hidden_units = w_gate.shape[1]
    as_float = in_rows.astype(jnp.float32)
    row_scale = lax.rsqrt(jnp.mean(as_float * as_float, axis=1, keepdims=True) + 1e-06)
    normed = (as_float * row_scale).astype(jnp.bfloat16)
    gate_act = jnp.dot(normed, w_gate, preferred_element_type=jnp.float32) * model_width ** (-0.5)
    up_act = jnp.dot(normed, w_up, preferred_element_type=jnp.float32) * model_width ** (-0.5)
    hidden = (jax.nn.silu(gate_act) * up_act).astype(jnp.bfloat16)
    branch = jnp.dot(hidden, w_down, preferred_element_type=jnp.float32) * hidden_units ** (-0.5)
    result = (as_float + branch).astype(jnp.bfloat16)
    return (result, (row_scale, gate_act, up_act, hidden))


def contract_last(left, right):
    return lax.dot_general(
        left, right, (((1,), (1,)), ((), ())), preferred_element_type=jnp.float32
    )


def grad_rows(cotangent, hidden, hidden_units):
    return lax.dot_general(
        hidden, cotangent, (((0,), (0,)), ((), ())), preferred_element_type=jnp.float32
    ) * hidden_units ** (-0.5)


def backward_rows(cotangent, in_rows, saved_state, w_gate, w_up, w_down):
    row_scale, gate_act, up_act, hidden = saved_state
    model_width = in_rows.shape[1]
    hidden_units = w_gate.shape[1]
    d_hidden = contract_last(cotangent, w_down) * hidden_units ** (-0.5)
    grad_term = grad_rows(cotangent, hidden, hidden_units)
    sigmoid_gate = jax.nn.sigmoid(gate_act)
    d_gate = (d_hidden * up_act * sigmoid_gate * (1.0 + gate_act * (1.0 - sigmoid_gate))).astype(
        jnp.bfloat16
    )
    d_up = (d_hidden * gate_act * sigmoid_gate).astype(jnp.bfloat16)
    d_normed = (contract_last(d_gate, w_gate) + contract_last(d_up, w_up)) * model_width ** (-0.5)
    as_float = in_rows.astype(jnp.float32)
    back_rows = (
        cotangent.astype(jnp.float32)
        + row_scale * d_normed
        - as_float * row_scale**3 * jnp.mean(d_normed * as_float, axis=1, keepdims=True)
    )
    return (grad_term, back_rows.astype(jnp.bfloat16))


def hop_kernel(flip, source, target, rows, out, send_sem, recv_sem):
    me, section = lax.axis_index("rep"), lax.axis_index("section")
    peer = me
    for bit in range(flip.bit_length()):
        if flip >> bit & 1:
            peer = peer + (1 << bit) - (2 << bit) * ((me // (1 << bit)) % 2)
    other = {"rep": peer, "section": section if source == target else 1 - section}
    barrier = pltpu.get_barrier_semaphore()
    pl.semaphore_signal(barrier, inc=1, device_id=other, device_id_type=pl.DeviceIdType.MESH)
    pl.semaphore_wait(barrier, 1)
    copy = pltpu.make_async_remote_copy(
        src_ref=rows, dst_ref=out, send_sem=send_sem, recv_sem=recv_sem,
        device_id=other, device_id_type=pl.DeviceIdType.MESH,
    )

    @pl.when(section == source)
    def _():
        copy.start()
        copy.wait_send()

    @pl.when(section == target)
    def _():
        copy.wait_recv()


def send_rows(payload, flip_key, source):
    bits = lax.axis_size("rep").bit_length() - 1
    starts = list(range(0, bits, 4))
    for index, start in enumerate(starts):
        width = min(4, bits - start)
        target = 1 - source if start == starts[-1] else source

        def branch(flip, index=index, start=start, target=target):
            if target == source and flip == 0:
                return lambda rows: rows
            in_vmem = pl.BlockSpec(memory_space=pltpu.VMEM)
            return pl.pallas_call(
                functools.partial(hop_kernel, flip << start, source, target),
                out_shape=jax.ShapeDtypeStruct(payload.shape, payload.dtype),
                in_specs=[in_vmem],
                out_specs=in_vmem,
                scratch_shapes=[pltpu.SemaphoreType.DMA, pltpu.SemaphoreType.DMA],
                compiler_params=pltpu.CompilerParams(
                    collective_id=1 + (index * 2 + source) * 16 + flip,
                    has_side_effects=True,
                    vmem_limit_bytes=4 * 1024 * 1024,
                ),
                name="hop",
            )

        payload = lax.switch(
            flip_key >> start & (1 << width) - 1, [branch(f) for f in range(1 << width)], payload
        )
    return payload


def outer_kernel(
    chunks, masks, grad, first_in, second_in, slow, mate_slow, momentum,
    new_slow, new_momentum, own, near, chosen, far, send_near, recv_near, send_far, recv_far,
):
    me = lax.axis_index("rep")
    peers = (me + 1 - 2 * (me % 2), me + 2 - 4 * ((me // 2) % 2))
    rows = grad.shape[0] // chunks
    f32, bf16 = jnp.float32, jnp.bfloat16

    barrier = pltpu.get_barrier_semaphore()
    for peer in peers:
        pl.semaphore_signal(
            barrier, inc=1, device_id={"rep": peer}, device_id_type=pl.DeviceIdType.MESH
        )

    def part(c):
        return pl.ds(pl.multiple_of(c * rows, rows), rows)

    def near_copy(c, order):
        return pltpu.make_async_remote_copy(
            src_ref=own.at[part(c)], dst_ref=near.at[part(c)],
            send_sem=send_near.at[c], recv_sem=recv_near.at[c],
            device_id={"rep": peers[order]}, device_id_type=pl.DeviceIdType.MESH,
        )

    def far_copy(c, order):
        return pltpu.make_async_remote_copy(
            src_ref=chosen.at[part(c)], dst_ref=far.at[part(c)],
            send_sem=send_far.at[c], recv_sem=recv_far.at[c],
            device_id={"rep": peers[1 - order]}, device_id_type=pl.DeviceIdType.MESH,
        )

    def adam(c):
        p = part(c)
        g = grad[p, :]
        first = 0.9 * first_in[p, :].astype(f32) + 0.1 * g
        second = 0.999 * second_in[p, :].astype(f32) + 0.001 * g * g
        step = first / (jnp.sqrt(second) + 1e-08)
        own[p, :] = (step + 0.1 * slow[p, :].astype(f32)).astype(bf16)

    def send(c, order):
        near_copy(c, order).start()

    def begin(c, order):
        adam(c)
        send(c, order)

    def pass_on(c, order):
        p = part(c)
        near_copy(c, order).wait_recv()
        chosen[p, :] = jnp.where(
            masks[order : order + 1, :] == 1, near[p, :].astype(f32), own[p, :].astype(f32)
        ).astype(bf16)
        far_copy(c, order).start()

    def finish(c, order):
        p = part(c)
        far_copy(c, order).wait_recv()
        mate = jnp.where(
            masks[1 - order : 2 - order, :] == 1, far[p, :].astype(f32), chosen[p, :].astype(f32)
        )
        mean = 0.5 * (own[p, :].astype(f32) + mate)
        moment = 0.9 * momentum[p, :].astype(f32) + mean
        averaged = 0.5 * (slow[p, :].astype(f32) + mate_slow[p, :].astype(f32))
        new_slow[p, :] = (averaged - 0.014 * (0.9 * moment + mean)).astype(bf16)
        new_momentum[p, :] = moment.astype(bf16)

    def settle(c, order):
        near_copy(c, order).wait_send()
        far_copy(c, order).wait_send()

    def both(start, stop, *stages):
        def run(pair, carry):
            for stage in stages:
                for order in range(2):
                    stage(2 * pair + order, order)
            return carry

        lax.fori_loop(start, stop, run, 0)

    pairs = chunks // 2
    both(0, 1, lambda c, order: adam(c))
    pl.semaphore_wait(barrier, 2)
    both(0, 1, send)
    both(1, pairs, begin)
    both(0, 1, pass_on)
    both(1, pairs, pass_on, lambda c, order: finish(c - 2, order))
    both(pairs - 1, pairs, finish)
    both(0, pairs, settle)


def outer_update(masks, grad, first_in, second_in, slow, mate_slow, momentum):
    hidden_units, model_width = grad.shape
    chunks = hidden_units // 32
    block = pltpu.VMEM((hidden_units, model_width), jnp.bfloat16)
    sems = pltpu.SemaphoreType.DMA((chunks,))
    out = jax.ShapeDtypeStruct((hidden_units, model_width), jnp.bfloat16)
    in_vmem = pl.BlockSpec(memory_space=pltpu.VMEM)
    return pl.pallas_call(
        functools.partial(outer_kernel, chunks),
        out_shape=(out, out),
        in_specs=[in_vmem] * 7,
        out_specs=(in_vmem, in_vmem),
        scratch_shapes=[block] * 4 + [sems] * 4,
        compiler_params=pltpu.CompilerParams(
            collective_id=0, has_side_effects=True, vmem_limit_bytes=16 * 1024 * 1024
        ),
        name="outer",
    )(masks, grad, first_in, second_in, slow, mate_slow, momentum)


def on_device(ends, w_gate, w_up, slow_down, adam_m, adam_v, momentum, routes, partner):
    micro_count, row_count, model_width = ends.shape[2:]
    own_data = ends.reshape(micro_count * row_count, model_width)
    gate_w = w_gate[0, 0]
    up_w = w_up[0, 0]
    down_w = slow_down[0, 0]
    hidden_units = gate_w.shape[1]
    replica = lax.axis_index("rep")
    on_first = lax.axis_index("section") == 0
    flip_keys = routes[:, 0]
    flip_bits = jnp.bitwise_xor(partner[replica], replica)
    near_slow = partner_2(down_w, "rep", 0)

    def cut(rows):
        return rows.reshape(micro_count, row_count, model_width)

    def first_forward():
        result, saved = forward_rows(own_data, gate_w, up_w, down_w)
        return result, saved[3]

    def first_idle():
        return own_data, jnp.zeros((own_data.shape[0], hidden_units), jnp.bfloat16)

    sent, hidden = lax.cond(on_first, first_forward, first_idle)
    sent = cut(sent)
    arrived = [send_rows(sent[b], flip_keys[b], 0) for b in range(micro_count)]
    near_slow, *arrived = lax.optimization_barrier((near_slow, *arrived))
    arrived = jnp.concatenate(arrived)
    chosen_slow = jnp.where(flip_bits & 1 == 1, near_slow, down_w)
    far_slow = partner_2(chosen_slow, "rep", 1)

    def last_work():
        _, saved = forward_rows(arrived, gate_w, up_w, down_w)
        term, back = backward_rows(own_data, arrived, saved, gate_w, up_w, down_w)
        return term, back

    def last_idle():
        return jnp.zeros((hidden_units, model_width), jnp.float32), own_data

    last_term, back = lax.cond(on_first, last_idle, last_work)
    back = cut(back)
    returned = [send_rows(back[b], flip_keys[b], 1) for b in range(micro_count)]
    far_slow, *returned = lax.optimization_barrier((far_slow, *returned))
    returned = jnp.concatenate(returned)
    partner_slow = jnp.where(flip_bits >> 1 & 1 == 1, far_slow, chosen_slow)
    grad_sum = lax.cond(
        on_first, lambda: grad_rows(returned, hidden, hidden_units), lambda: last_term
    )
    masks = jnp.zeros((8, model_width), jnp.int32)
    masks = masks.at[0].set(flip_bits & 1).at[1].set(flip_bits >> 1 & 1)
    new_slow, new_momentum = outer_update(
        masks, grad_sum, adam_m[0, 0], adam_v[0, 0], down_w, partner_slow, momentum[0, 0]
    )
    return new_slow[None, None], new_momentum[None, None]


def solution(mesh):
    placed = (
        P("section", "rep", None, None, None),
        P("section", "rep", None, None),
        P("section", "rep", None, None),
        P("section", "rep", None, None),
        P("section", "rep", None, None),
        P("section", "rep", None, None),
        P("section", "rep", None, None),
        P(),
        P(),
    )

    return jax.shard_map(
        on_device,
        mesh=mesh,
        in_specs=placed,
        out_specs=(P("section", "rep", None, None), P("section", "rep", None, None)),
        check_vma=False,
    )
```

```python
import functools

import jax
import jax.numpy as jnp
from jax import lax
from jax.experimental import pallas as pl
from jax.experimental.pallas import tpu as pltpu
from jax.sharding import PartitionSpec as P


def partner_2(x, axis, bit):
    return lax.ppermute(x, axis, [(i, i ^ 1 << bit) for i in range(lax.axis_size(axis))])


def forward_rows(in_rows, w_gate, w_up, w_down):
    model_width = in_rows.shape[1]
    hidden_units = w_gate.shape[1]
    as_float = in_rows.astype(jnp.float32)
    row_scale = lax.rsqrt(jnp.mean(as_float * as_float, axis=1, keepdims=True) + 1e-06)
    normed = (as_float * row_scale).astype(jnp.bfloat16)
    gate_act = jnp.dot(normed, w_gate, preferred_element_type=jnp.float32) * model_width ** (-0.5)
    up_act = jnp.dot(normed, w_up, preferred_element_type=jnp.float32) * model_width ** (-0.5)
    hidden = (jax.nn.silu(gate_act) * up_act).astype(jnp.bfloat16)
    branch = jnp.dot(hidden, w_down, preferred_element_type=jnp.float32) * hidden_units ** (-0.5)
    result = (as_float + branch).astype(jnp.bfloat16)
    return (result, (row_scale, gate_act, up_act, hidden))


def contract_last(left, right):
    return lax.dot_general(
        left, right, (((1,), (1,)), ((), ())), preferred_element_type=jnp.float32
    )


def grad_rows(cotangent, hidden, hidden_units):
    return lax.dot_general(
        hidden, cotangent, (((0,), (0,)), ((), ())), preferred_element_type=jnp.float32
    ) * hidden_units ** (-0.5)


def backward_rows(cotangent, in_rows, saved_state, w_gate, w_up, w_down):
    row_scale, gate_act, up_act, hidden = saved_state
    model_width = in_rows.shape[1]
    hidden_units = w_gate.shape[1]
    d_hidden = contract_last(cotangent, w_down) * hidden_units ** (-0.5)
    grad_term = grad_rows(cotangent, hidden, hidden_units)
    sigmoid_gate = jax.nn.sigmoid(gate_act)
    d_gate = (d_hidden * up_act * sigmoid_gate * (1.0 + gate_act * (1.0 - sigmoid_gate))).astype(
        jnp.bfloat16
    )
    d_up = (d_hidden * gate_act * sigmoid_gate).astype(jnp.bfloat16)
    d_normed = (contract_last(d_gate, w_gate) + contract_last(d_up, w_up)) * model_width ** (-0.5)
    as_float = in_rows.astype(jnp.float32)
    back_rows = (
        cotangent.astype(jnp.float32)
        + row_scale * d_normed
        - as_float * row_scale**3 * jnp.mean(d_normed * as_float, axis=1, keepdims=True)
    )
    return (grad_term, back_rows.astype(jnp.bfloat16))


def hop_kernel(flip, source, target, rows, out, send_sem, recv_sem):
    me, section = lax.axis_index("rep"), lax.axis_index("section")
    peer = me
    for bit in range(flip.bit_length()):
        if flip >> bit & 1:
            peer = peer + (1 << bit) - (2 << bit) * ((me // (1 << bit)) % 2)
    other = {"rep": peer, "section": section if source == target else 1 - section}
    barrier = pltpu.get_barrier_semaphore()
    pl.semaphore_signal(barrier, inc=1, device_id=other, device_id_type=pl.DeviceIdType.MESH)
    pl.semaphore_wait(barrier, 1)
    copy = pltpu.make_async_remote_copy(
        src_ref=rows, dst_ref=out, send_sem=send_sem, recv_sem=recv_sem,
        device_id=other, device_id_type=pl.DeviceIdType.MESH,
    )

    @pl.when(section == source)
    def _():
        copy.start()
        copy.wait_send()

    @pl.when(section == target)
    def _():
        copy.wait_recv()


def send_rows(payload, flip_key, source):
    bits = lax.axis_size("rep").bit_length() - 1
    starts = list(range(0, bits, 4))
    for index, start in enumerate(starts):
        width = min(4, bits - start)
        target = 1 - source if start == starts[-1] else source

        def branch(flip, index=index, start=start, target=target):
            if target == source and flip == 0:
                return lambda rows: rows
            in_vmem = pl.BlockSpec(memory_space=pltpu.VMEM)
            return pl.pallas_call(
                functools.partial(hop_kernel, flip << start, source, target),
                out_shape=jax.ShapeDtypeStruct(payload.shape, payload.dtype),
                in_specs=[in_vmem],
                out_specs=in_vmem,
                scratch_shapes=[pltpu.SemaphoreType.DMA, pltpu.SemaphoreType.DMA],
                compiler_params=pltpu.CompilerParams(
                    collective_id=1 + (index * 2 + source) * 16 + flip,
                    has_side_effects=True,
                    vmem_limit_bytes=4 * 1024 * 1024,
                ),
                name="hop",
            )

        payload = lax.switch(
            flip_key >> start & (1 << width) - 1, [branch(f) for f in range(1 << width)], payload
        )
    return payload


def twin_kernel(flips, source, rows, out, send_sem, recv_sem):
    me, section = lax.axis_index("rep"), lax.axis_index("section")
    others = []
    for flip in flips:
        peer = me
        for bit in range(flip.bit_length()):
            if flip >> bit & 1:
                peer = peer + (1 << bit) - (2 << bit) * ((me // (1 << bit)) % 2)
        others.append({"rep": peer, "section": 1 - section})
    barrier = pltpu.get_barrier_semaphore()
    for other in others:
        pl.semaphore_signal(barrier, inc=1, device_id=other, device_id_type=pl.DeviceIdType.MESH)
    pl.semaphore_wait(barrier, 2)
    copies = [
        pltpu.make_async_remote_copy(
            src_ref=rows.at[b], dst_ref=out.at[b], send_sem=send_sem.at[b],
            recv_sem=recv_sem.at[b], device_id=others[b],
            device_id_type=pl.DeviceIdType.MESH,
        )
        for b in range(2)
    ]

    @pl.when(section == source)
    def _():
        for copy in copies:
            copy.start()
        for copy in copies:
            copy.wait_send()

    @pl.when(section != source)
    def _():
        for copy in copies:
            copy.wait_recv()


def send_batches(payload, flip_keys, source):
    replicas = lax.axis_size("rep")
    if payload.shape[0] != 2 or replicas > 16:
        return jnp.stack(
            [send_rows(payload[b], flip_keys[b], source) for b in range(payload.shape[0])]
        )
    in_vmem = pl.BlockSpec(memory_space=pltpu.VMEM)
    span = replicas - 1

    flips = [(low + 1, high + 1) for high in range(span) for low in range(high + 1)]

    def branch(index):
        return pl.pallas_call(
            functools.partial(twin_kernel, flips[index], source),
            out_shape=jax.ShapeDtypeStruct(payload.shape, payload.dtype),
            in_specs=[in_vmem],
            out_specs=in_vmem,
            scratch_shapes=[pltpu.SemaphoreType.DMA((2,)), pltpu.SemaphoreType.DMA((2,))],
            compiler_params=pltpu.CompilerParams(
                collective_id=1 + source * len(flips) + index,
                has_side_effects=True,
                vmem_limit_bytes=4 * 1024 * 1024,
            ),
            name="twin",
        )

    return lax.switch(
        flip_keys[1] * (flip_keys[1] - 1) // 2 + flip_keys[0] - 1,
        [branch(index) for index in range(len(flips))],
        payload,
    )


def outer_kernel(
    chunks, masks, grad, first_in, second_in, slow, mate_slow, momentum,
    new_slow, new_momentum, own, near, chosen, far, send_near, recv_near, send_far, recv_far,
):
    me = lax.axis_index("rep")
    peers = (me + 1 - 2 * (me % 2), me + 2 - 4 * ((me // 2) % 2))
    rows = grad.shape[0] // chunks
    f32, bf16 = jnp.float32, jnp.bfloat16

    barrier = pltpu.get_barrier_semaphore()
    for peer in peers:
        pl.semaphore_signal(
            barrier, inc=1, device_id={"rep": peer}, device_id_type=pl.DeviceIdType.MESH
        )

    def part(c):
        return pl.ds(pl.multiple_of(c * rows, rows), rows)

    def near_copy(c, order):
        return pltpu.make_async_remote_copy(
            src_ref=own.at[part(c)], dst_ref=near.at[part(c)],
            send_sem=send_near.at[c], recv_sem=recv_near.at[c],
            device_id={"rep": peers[order]}, device_id_type=pl.DeviceIdType.MESH,
        )

    def far_copy(c, order):
        return pltpu.make_async_remote_copy(
            src_ref=chosen.at[part(c)], dst_ref=far.at[part(c)],
            send_sem=send_far.at[c], recv_sem=recv_far.at[c],
            device_id={"rep": peers[1 - order]}, device_id_type=pl.DeviceIdType.MESH,
        )

    def adam(c):
        p = part(c)
        g = grad[p, :]
        first = 0.9 * first_in[p, :].astype(f32) + 0.1 * g
        second = 0.999 * second_in[p, :].astype(f32) + 0.001 * g * g
        step = first / (jnp.sqrt(second) + 1e-08)
        own[p, :] = (step + 0.1 * slow[p, :].astype(f32)).astype(bf16)

    def send(c, order):
        near_copy(c, order).start()

    def begin(c, order):
        adam(c)
        send(c, order)

    def pass_on(c, order):
        p = part(c)
        near_copy(c, order).wait_recv()
        chosen[p, :] = jnp.where(
            masks[order : order + 1, :] == 1, near[p, :].astype(f32), own[p, :].astype(f32)
        ).astype(bf16)
        far_copy(c, order).start()

    def finish(c, order):
        p = part(c)
        far_copy(c, order).wait_recv()
        mate = jnp.where(
            masks[1 - order : 2 - order, :] == 1, far[p, :].astype(f32), chosen[p, :].astype(f32)
        )
        mean = 0.5 * (own[p, :].astype(f32) + mate)
        moment = 0.9 * momentum[p, :].astype(f32) + mean
        averaged = 0.5 * (slow[p, :].astype(f32) + mate_slow[p, :].astype(f32))
        new_slow[p, :] = (averaged - 0.014 * (0.9 * moment + mean)).astype(bf16)
        new_momentum[p, :] = moment.astype(bf16)

    def settle(c, order):
        near_copy(c, order).wait_send()
        far_copy(c, order).wait_send()

    def both(start, stop, *stages):
        def run(pair, carry):
            for stage in stages:
                for order in range(2):
                    stage(2 * pair + order, order)
            return carry

        lax.fori_loop(start, stop, run, 0)

    pairs = chunks // 2
    both(0, 1, lambda c, order: adam(c))
    pl.semaphore_wait(barrier, 2)
    both(0, 1, send)
    both(1, pairs, begin)
    both(0, 1, pass_on)
    both(1, pairs, pass_on, lambda c, order: finish(c - 2, order))
    both(pairs - 1, pairs, finish)
    both(0, pairs, settle)


def outer_update(masks, grad, first_in, second_in, slow, mate_slow, momentum):
    hidden_units, model_width = grad.shape
    chunks = hidden_units // 32
    block = pltpu.VMEM((hidden_units, model_width), jnp.bfloat16)
    sems = pltpu.SemaphoreType.DMA((chunks,))
    out = jax.ShapeDtypeStruct((hidden_units, model_width), jnp.bfloat16)
    in_vmem = pl.BlockSpec(memory_space=pltpu.VMEM)
    return pl.pallas_call(
        functools.partial(outer_kernel, chunks),
        out_shape=(out, out),
        in_specs=[in_vmem] * 7,
        out_specs=(in_vmem, in_vmem),
        scratch_shapes=[block] * 4 + [sems] * 4,
        compiler_params=pltpu.CompilerParams(
            collective_id=0, has_side_effects=True, vmem_limit_bytes=16 * 1024 * 1024
        ),
        name="outer",
    )(masks, grad, first_in, second_in, slow, mate_slow, momentum)


def on_device(ends, w_gate, w_up, slow_down, adam_m, adam_v, momentum, routes, partner):
    micro_count, row_count, model_width = ends.shape[2:]
    flip_keys = routes[:, 0]
    own_data = ends[0, 0]
    if micro_count == 2:
        own_data = jnp.where(flip_keys[0] > flip_keys[1], own_data[::-1], own_data)
        flip_keys = jnp.stack([jnp.min(flip_keys), jnp.max(flip_keys)])
    own_data = own_data.reshape(micro_count * row_count, model_width)
    gate_w = w_gate[0, 0]
    up_w = w_up[0, 0]
    down_w = slow_down[0, 0]
    hidden_units = gate_w.shape[1]
    replica = lax.axis_index("rep")
    on_first = lax.axis_index("section") == 0
    flip_bits = jnp.bitwise_xor(partner[replica], replica)
    near_slow = partner_2(down_w, "rep", 0)

    def cut(rows):
        return rows.reshape(micro_count, row_count, model_width)

    def first_forward():
        result, saved = forward_rows(own_data, gate_w, up_w, down_w)
        return result, saved[3]

    def first_idle():
        return own_data, jnp.zeros((own_data.shape[0], hidden_units), jnp.bfloat16)

    sent, hidden = lax.cond(on_first, first_forward, first_idle)
    sent = cut(sent)
    arrived = send_batches(sent, flip_keys, 0)
    near_slow, arrived = lax.optimization_barrier((near_slow, arrived))
    arrived = arrived.reshape(own_data.shape)
    chosen_slow = jnp.where(flip_bits & 1 == 1, near_slow, down_w)
    far_slow = partner_2(chosen_slow, "rep", 1)

    def last_work():
        _, saved = forward_rows(arrived, gate_w, up_w, down_w)
        term, back = backward_rows(own_data, arrived, saved, gate_w, up_w, down_w)
        return term, back

    def last_idle():
        return jnp.zeros((hidden_units, model_width), jnp.float32), own_data

    last_term, back = lax.cond(on_first, last_idle, last_work)
    back = cut(back)
    returned = send_batches(back, flip_keys, 1)
    far_slow, returned = lax.optimization_barrier((far_slow, returned))
    returned = returned.reshape(own_data.shape)
    partner_slow = jnp.where(flip_bits >> 1 & 1 == 1, far_slow, chosen_slow)
    grad_sum = lax.cond(
        on_first, lambda: grad_rows(returned, hidden, hidden_units), lambda: last_term
    )
    masks = jnp.zeros((8, model_width), jnp.int32)
    masks = masks.at[0].set(flip_bits & 1).at[1].set(flip_bits >> 1 & 1)
    new_slow, new_momentum = outer_update(
        masks, grad_sum, adam_m[0, 0], adam_v[0, 0], down_w, partner_slow, momentum[0, 0]
    )
    return new_slow[None, None], new_momentum[None, None]


def solution(mesh):
    placed = (
        P("section", "rep", None, None, None),
        P("section", "rep", None, None),
        P("section", "rep", None, None),
        P("section", "rep", None, None),
        P("section", "rep", None, None),
        P("section", "rep", None, None),
        P("section", "rep", None, None),
        P(),
        P(),
    )

    return jax.shard_map(
        on_device,
        mesh=mesh,
        in_specs=placed,
        out_specs=(P("section", "rep", None, None), P("section", "rep", None, None)),
        check_vma=False,
    )
```
